32 devices in a mesh: groups: 2 (over y), item: 4 (over z), dp: 2 (over core), tensor: 2 (over x).
Axes of the slice: x: 2, y: 2, z: 4, core: 2. Of those that a mesh axis runs over, the one named last changes fastest.
Arguments:
- events: bfloat16 [12288, 1024], P(('groups', 'item', 'dp')), parts along dimension 0, may hold values from -6 to 6
- lengths: int32 [16], P('groups'), parts along dimension 0, may hold values from 192 to 768, as said below
- packing: int32 [16], P('groups'), parts along dimension 0, may hold values from 0 to 7, each once
- positions: int32 [16, 64], P('groups'), parts along dimension 0, may hold values from 0 to 767, as said below
- logged: int32 [16, 64], P('groups'), parts along dimension 0, may hold values from 0 to 16383
- w_uvqk: bfloat16 [1024, 1024], P(None, 'tensor'), may hold values from -0.1875 to 0.1875
- w_out: bfloat16 [256, 1024], P('tensor'), may hold values from -0.375 to 0.375
- catalogue: bfloat16 [16384, 1024], P(('item', 'dp', 'tensor')), may hold values from -0.46875 to 0.46875
Outputs:
- scoring_state: bfloat16 [1024, 1024], P(('groups', 'item', 'dp'), 'tensor'), parts along dimension 0
- log_propensity: float32 [1024], P(('groups', 'item', 'dp')), parts along dimension 0
The draws below stay inside these ranges and needn't reach their ends.
There are 2 independent parts, one for each index of `groups`. The reference program is written for one: setup_inputs(seed, part) draws one part's arguments, and reference() takes and returns one part's arrays. A program takes and returns all parts, laid end to end along the dimension named above; an argument that names none is the same for every part. Nothing has to cross between parts.
Inputs may be any that keep to these rules, and one draw needn't show every extreme that they name: `lengths`: one history has exactly 768 valid events and one exactly 192. positions[h, k] < lengths[h]. `packing`: each history id appears once.
All inputs are finite; a program needn't handle non-finite values.
Results may differ from the reference program's by a relative error of at most 0.0048.
Values may be sent and summed in bfloat16 or wider, within the bound.
A program may use at most 64 MiB of HBM per device.

```python
import math
import jax
import jax.numpy as jnp
import numpy as np
from jax import lax

D = 1024
DH = 128
SLOT = 768
IMP_DEV = 64
ITEM_DEV = 1024
HEADS = 2
NHIST = 8
ITEMS = 16384
N_TENSOR = 2


def lengths_of(key):
    drawn = jax.random.randint(jax.random.fold_in(key, 11), (NHIST,), SLOT // 4, SLOT + 1)
    longest = jax.random.randint(jax.random.fold_in(key, 12), (), 0, NHIST)
    hist_index = jnp.arange(NHIST)
    drawn = jnp.where(hist_index == longest, SLOT, drawn)
    drawn = jnp.where(hist_index == (longest + 1) % NHIST, SLOT // 4, drawn)
    return (drawn.astype(jnp.int32), longest)


def draw_lengths(key, part):
    return lengths_of(key)[0]


def draw_positions(key, part):
    hist_lengths, longest = lengths_of(key)
    event_spots = jax.random.randint(jax.random.fold_in(key, 13), (NHIST, IMP_DEV), 0, hist_lengths[:, None])
    row_index = jnp.arange(NHIST)[:, None]
    col_index = jnp.arange(IMP_DEV)[None, :]
    event_spots = jnp.where((row_index == longest) & (col_index == 0), SLOT - 1, event_spots)
    event_spots = jnp.where((row_index == longest) & (col_index == 1), 0, event_spots)
    return event_spots.astype(jnp.int32)


def draw_events(key, part):
    shape = (NHIST * SLOT, D)
    values = jnp.clip(jax.random.normal(jax.random.fold_in(key, 22), shape, jnp.float32), -6.0, 6.0)
    return values.astype(jnp.bfloat16)


def draw_catalogue(key, part):
    shape = (ITEMS, D)
    scale = 1.0 / D ** 0.5
    values = jnp.clip(jax.random.normal(jax.random.fold_in(key, 32), shape, jnp.float32) * 2.5, -15.0, 15.0) * scale
    return values.astype(jnp.bfloat16)


def set_ends(entries, stream_key, smallest, largest):
    place = [jax.random.randint(jax.random.fold_in(stream_key, axis), (), 0, length) for axis, length in enumerate(entries.shape)]
    widest = entries.shape.index(max(entries.shape))
    neighbour = place[:widest] + [(place[widest] + 1) % entries.shape[widest]] + place[widest + 1:]
    return entries.at[tuple(place)].set(smallest).at[tuple(neighbour)].set(largest)


def block_levels(rng, extent, shards, least, largest):
    def one(axis_at, shards_of):
        heights = jax.random.uniform(jax.random.fold_in(jax.random.fold_in(rng, 6), axis_at), (shards_of,), jnp.float32, least / len(shards), largest / len(shards))
        return jnp.repeat(jnp.exp(heights), extent[axis_at] // shards_of).reshape((-1,) + (1,) * (len(extent) - axis_at - 1))

    gain = one(*shards[0])
    for cut in shards[1:]:
        gain = gain * one(*cut)
    return gain


def rank_bounds(number_of, lean):
    portions = [(1 << 20) // math.isqrt(grade ** lean) + 1 for grade in range(1, number_of + 1)]
    spread = 1 + sum(portions) // (1 << 30)
    return np.cumsum(np.array([max(1, weight // spread) for weight in portions]))


def skewed_ids(key, extent, amount, skew):
    listing = rank_bounds(amount, skew)
    ticket = jax.random.randint(jax.random.fold_in(key, 1), extent, 0, int(listing[amount - 1]))
    grade = jnp.searchsorted(jnp.asarray(listing, jnp.int32), ticket, side="right")
    return jax.random.permutation(jax.random.fold_in(key, 2), amount)[grade].astype(jnp.int32)


def noise(key, shape, deviation, reach, split=(), held_as=jnp.bfloat16):
    gain = block_levels(key, shape, split, -0.22, 0.18) if split else 1.0
    values = jax.random.normal(key, shape, jnp.float32) * deviation * gain
    return jnp.minimum(jnp.maximum(values, -reach), reach).astype(held_as)


def setup_inputs(seed: int = 0, part: int = 0) -> dict:
    seeds = jax.random.split(jax.random.key(seed), 9)
    part_splits = jax.random.split(jax.random.fold_in(seeds[8], part), 9)
    return {
        "events": draw_events(jax.random.fold_in(jax.random.fold_in(seeds[8], part), 71), part),
        "lengths": draw_lengths(jax.random.fold_in(jax.random.fold_in(seeds[8], part), 71), part),
        "packing": jax.random.permutation(part_splits[2], NHIST).astype(jnp.int32),
        "positions": draw_positions(jax.random.fold_in(jax.random.fold_in(seeds[8], part), 71), part),
        "logged": set_ends(skewed_ids(part_splits[4], (NHIST, IMP_DEV), ITEMS, 2), jax.random.fold_in(part_splits[4], 3), 0, ITEMS - 1).astype(jnp.int32),
        "w_uvqk": noise(seeds[5], (D, HEADS * 4 * DH), D ** -0.5, 0.1875, ((1, 2),)),
        "w_out": noise(seeds[6], (HEADS * DH, D), (HEADS * DH) ** -0.5, 0.375, ((0, 2),)),
        "catalogue": draw_catalogue(jax.random.fold_in(seeds[8], 71), part),
    }


def score_slot(slot_events, hist_length, event_spots, w_uvqk, w_out):
    projected = jnp.dot(slot_events, w_uvqk, preferred_element_type=jnp.float32)
    projected = jax.nn.silu(projected).astype(jnp.bfloat16).reshape(SLOT, HEADS, 4, DH)
    chosen_proj = jnp.take(projected, event_spots, axis=0).astype(jnp.float32)
    keys_values = projected.astype(jnp.float32)
    scores = jnp.einsum('ied,med->iem', chosen_proj[:, :, 2], keys_values[:, :, 3]) / math.sqrt(DH)
    slot_range = jnp.arange(SLOT).astype(jnp.int32)
    is_valid = (slot_range[None, :] <= event_spots[:, None]) & (slot_range[None, :] < hist_length)
    weights = jnp.where(is_valid[:, None, :], jax.nn.silu(scores), 0.0).astype(jnp.bfloat16)
    attended = jnp.einsum('iem,med->ied', weights.astype(jnp.float32), keys_values[:, :, 1])
    inverse = lax.rsqrt(lax.optimization_barrier(jnp.mean(attended * attended, axis=-1, keepdims=True)) + 1e-06)
    gated_rows = (attended * inverse * chosen_proj[:, :, 0]).astype(jnp.bfloat16)
    gated_rows = gated_rows.reshape(IMP_DEV, HEADS * DH)
    mixed = jnp.dot(gated_rows, w_out, preferred_element_type=jnp.float32)
    mixed = mixed + jnp.take(slot_events, event_spots, axis=0).astype(jnp.float32)
    return mixed.astype(jnp.bfloat16)

def reference(events, lengths, packing, positions, logged, w_uvqk, w_out, catalogue):
    slot_lengths = jnp.take(lengths, packing)
    slot_spots = jnp.take(positions, packing, axis=0)
    slot_items = jnp.take(logged, packing, axis=0).reshape(NHIST * IMP_DEV)
    grouped = events.reshape(NHIST, SLOT, D)

    def one_slot(inputs):
        return score_slot(inputs[0], inputs[1], inputs[2], w_uvqk, w_out)
    states = lax.map(one_slot, (grouped, slot_lengths, slot_spots)).reshape(NHIST * IMP_DEV, D)
    block_size = ITEM_DEV * N_TENSOR
    block_count = ITEMS // block_size
    blocks = catalogue.reshape(block_count, block_size, D)
    bases = (jnp.arange(block_count) * block_size).astype(jnp.int32)
    state_values = states.astype(jnp.float32)

    def step(running, inputs):
        block, item_base = inputs
        logits = jnp.dot(state_values, block.astype(jnp.float32).T, precision=lax.Precision.HIGHEST)
        local_ids = slot_items - item_base
        inside = (local_ids >= 0) & (local_ids < block_size)
        clipped = jnp.clip(local_ids, 0, block_size - 1).astype(jnp.int32)
        picked = jnp.take_along_axis(logits, clipped[:, None], axis=1)[:, 0]
        new_totals = running[0] + lax.optimization_barrier(jnp.sum(jnp.exp(logits), axis=1))
        new_target = running[1] + jnp.where(inside, picked, 0.0)
        return ((new_totals, new_target), None)
    initial = (jnp.zeros((NHIST * IMP_DEV,), jnp.float32), jnp.zeros((NHIST * IMP_DEV,), jnp.float32))
    finals, unused = lax.scan(step, initial, (blocks, bases))
    return (states, finals[1] - jnp.log(finals[0]))
```

```python
import functools
import math

import jax
import jax.numpy as jnp
from jax import lax
from jax.experimental import pallas as pl
from jax.experimental.pallas import tpu as pltpu
from jax.sharding import PartitionSpec as P

DH = 128
LANES = 128
ITEM_BLOCK = 256
MESH = pl.DeviceIdType.MESH


def silu(x):
    return x / (1.0 + jnp.exp(-x))


def kernel(
    nz,
    nt,
    packing,
    lengths,
    positions,
    logged,
    events_hbm,
    w_hbm,
    w_out_hbm,
    cat_hbm,
    state_out,
    prop_out,
    events,
    w_vk,
    w_uq,
    w_full,
    cat,
    chosen_all,
    gated_all,
    states,
    ids,
    stage,
    stats,
    load_sem,
    z_send,
    z_recv,
    sib_send,
    sib_recv,
    g_send,
    g_recv,
    gs_send,
    gs_recv,
    w_send,
    w_recv,
    s_send,
    s_recv,
):
    z = lax.axis_index("item")
    c = lax.axis_index("dp")
    t = lax.axis_index("tensor")
    slot = z * 2 + c
    imps = positions.shape[1]
    rows, width = events.shape
    nslots = nz * 2
    nlines = nz * nt
    ndev = nlines * 2
    line = z * nt + t
    me = slot * nt + t

    def device(lin):
        peer_slot = lin // nt
        return {"item": peer_slot // 2, "dp": lax.rem(peer_slot, 2), "tensor": lax.rem(lin, nt)}

    loads = [
        pltpu.make_async_copy(events_hbm, events, load_sem.at[0]),
        pltpu.make_async_copy(w_hbm.at[:, 0:DH], w_uq.at[:, 0:DH], load_sem.at[1]),
        pltpu.make_async_copy(w_hbm.at[:, 2 * DH : 3 * DH], w_uq.at[:, DH : 2 * DH], load_sem.at[2]),
        pltpu.make_async_copy(w_hbm.at[:, DH : 2 * DH], w_vk.at[:, 0:DH], load_sem.at[3]),
        pltpu.make_async_copy(w_hbm.at[:, 3 * DH : 4 * DH], w_vk.at[:, DH : 2 * DH], load_sem.at[4]),
        pltpu.make_async_copy(w_out_hbm, w_full.at[pl.ds(pl.multiple_of(t * DH, DH), DH), :], load_sem.at[5]),
        pltpu.make_async_copy(cat_hbm, cat, load_sem.at[6]),
    ]
    for copy in loads:
        copy.start()

    barrier = pltpu.get_barrier_semaphore()

    def greet(r, carry):
        pl.semaphore_signal(
            barrier, inc=1, device_id=device(lax.rem(me + r, ndev)), device_id_type=MESH
        )
        return carry

    lax.fori_loop(1, ndev, greet, 0)

    hist = packing[slot]
    length = lengths[hist].astype(jnp.float32)
    pos_row = positions[pl.ds(hist, 1), :].astype(jnp.float32)
    eye = lax.broadcasted_iota(jnp.int32, (imps, imps), 0) == lax.broadcasted_iota(
        jnp.int32, (imps, imps), 1
    )
    pos_col = jnp.sum(jnp.where(eye, pos_row, 0.0), axis=1, keepdims=True)
    spots = lax.broadcasted_iota(jnp.int32, (imps, rows), 1).astype(jnp.float32)
    pick = jnp.where(spots == pos_col, 1.0, 0.0).astype(jnp.bfloat16)
    for j in range(nslots):
        ids[0:1, j * imps : (j + 1) * imps] = logged[pl.ds(packing[j], 1), :]

    def rows_of(which):
        return pl.ds(pl.multiple_of(which * imps, imps), imps)

    loads[0].wait()
    chosen = jnp.dot(pick, events[...], preferred_element_type=jnp.float32).astype(jnp.bfloat16)
    chosen_all[rows_of(slot), :] = chosen
    pl.semaphore_wait(barrier, ndev - 1)

    def z_copy(r, source_slot):
        return pltpu.make_async_remote_copy(
            src_ref=chosen_all.at[rows_of(source_slot), :],
            dst_ref=chosen_all.at[rows_of(source_slot), :],
            send_sem=z_send.at[r],
            recv_sem=z_recv.at[r],
            device_id={"item": lax.rem(z + r, nz)},
            device_id_type=MESH,
        )

    def sib_copy(r, source_slot):
        return pltpu.make_async_remote_copy(
            src_ref=chosen_all.at[rows_of(source_slot), :],
            dst_ref=chosen_all.at[rows_of(source_slot), :],
            send_sem=sib_send.at[r],
            recv_sem=sib_recv.at[r],
            device_id={"dp": 1 - c},
            device_id_type=MESH,
        )

    def head_cols(which):
        return pl.ds(pl.multiple_of(which * DH, DH), DH)

    def w_copy(r, source_t):
        return pltpu.make_async_remote_copy(
            src_ref=w_out_hbm,
            dst_ref=w_full.at[head_cols(source_t), :],
            send_sem=w_send.at[r],
            recv_sem=w_recv.at[r],
            device_id={"tensor": lax.rem(t + r, nt)},
            device_id_type=MESH,
        )

    def gated_at(source_slot, source_t):
        return gated_all.at[rows_of(source_slot), head_cols(source_t)]

    def g_copy(r, source_slot, source_t):
        peer = lax.rem(line + r, nlines)
        return pltpu.make_async_remote_copy(
            src_ref=gated_at(source_slot, source_t),
            dst_ref=gated_at(source_slot, source_t),
            send_sem=g_send.at[r],
            recv_sem=g_recv.at[r],
            device_id={"item": peer // nt, "tensor": lax.rem(peer, nt)},
            device_id_type=MESH,
        )

    def gs_copy(r, source_slot, source_t):
        return pltpu.make_async_remote_copy(
            src_ref=gated_at(source_slot, source_t),
            dst_ref=gated_at(source_slot, source_t),
            send_sem=gs_send.at[r],
            recv_sem=gs_recv.at[r],
            device_id={"dp": 1 - c},
            device_id_type=MESH,
        )

    def loop(first, count, body):
        def step(r, carry):
            body(r)
            return carry

        lax.fori_loop(first, count, step, 0)

    loop(1, nz, lambda r: z_copy(r, slot).start())
    sib_copy(0, slot).start()
    loop(1, nt, lambda r: w_copy(r, t).start())

    loads[1].wait()
    loads[2].wait()
    gate_query = silu(
        jnp.dot(chosen, w_uq[...], preferred_element_type=jnp.float32)
    ).astype(jnp.bfloat16)
    loads[3].wait()
    loads[4].wait()
    values_keys = silu(
        jnp.dot(events[...], w_vk[...], preferred_element_type=jnp.float32)
    ).astype(jnp.bfloat16)
    scores = lax.dot_general(
        gate_query[:, DH:],
        values_keys[:, DH:],
        (((1,), (1,)), ((), ())),
        preferred_element_type=jnp.float32,
    ) * (1.0 / math.sqrt(DH))
    is_valid = (spots <= pos_col) & (spots < length)
    weights = jnp.where(is_valid, silu(scores), 0.0).astype(jnp.bfloat16)
    attended = jnp.dot(weights, values_keys[:, :DH], preferred_element_type=jnp.float32)
    inverse = lax.rsqrt(jnp.mean(attended * attended, axis=-1, keepdims=True) + 1e-06)
    gated = (attended * inverse * gate_query[:, :DH].astype(jnp.float32)).astype(jnp.bfloat16)
    gated_all[rows_of(slot), head_cols(t)] = gated

    loop(1, nlines, lambda r: g_copy(r, slot, t).start())
    gs_copy(0, slot, t).start()

    def z_source(r):
        return lax.rem(z + nz - r, nz) * 2

    def pass_chosen(r):
        z_copy(r, z_source(r) + c).wait_recv()
        sib_copy(r, z_source(r) + c).start()

    loop(1, nz, pass_chosen)

    def line_source(r):
        source = lax.rem(line + nlines - r, nlines)
        return (source // nt) * 2, lax.rem(source, nt)

    def pass_gated(r):
        base, source_t = line_source(r)
        g_copy(r, base + c, source_t).wait_recv()
        gs_copy(r, base + c, source_t).start()

    loop(1, nlines, pass_gated)

    loads[5].wait()
    loads[6].wait()
    loop(1, nt, lambda r: w_copy(r, lax.rem(t + nt - r, nt)).wait_recv())
    loop(0, nz, lambda r: sib_copy(r, z_source(r) + 1 - c).wait_recv())

    def take_gated(r):
        base, source_t = line_source(r)
        gs_copy(r, base + 1 - c, source_t).wait_recv()

    loop(0, nlines, take_gated)

    states[...] = (
        jnp.dot(gated_all[...], w_full[...], preferred_element_type=jnp.float32)
        + chosen_all[...].astype(jnp.float32)
    ).astype(jnp.bfloat16)
    share = width // nt
    state_out[...] = states[rows_of(slot), pl.ds(pl.multiple_of(t * share, LANES), share)]

    items = cat.shape[0]
    item_ids = ids[...]

    def block(b, carry):
        totals, target = carry
        logits = lax.dot_general(
            cat[pl.ds(pl.multiple_of(b * ITEM_BLOCK, ITEM_BLOCK), ITEM_BLOCK), :],
            states[...],
            (((1,), (1,)), ((), ())),
            preferred_element_type=jnp.float32,
        )
        local = item_ids - (me * items + b * ITEM_BLOCK)
        matches = lax.broadcasted_iota(jnp.int32, logits.shape, 0) == local
        totals = totals + jnp.sum(jnp.exp(logits), axis=0, keepdims=True)
        target = target + jnp.sum(jnp.where(matches, logits, 0.0), axis=0, keepdims=True)
        return totals, target

    zero = jnp.zeros((1, nslots * imps), jnp.float32)
    totals, target = lax.fori_loop(0, items // ITEM_BLOCK, block, (zero, zero))
    upper = lax.broadcasted_iota(jnp.int32, (8, LANES), 0) < 4
    for j in range(nz):
        cut = slice(j * LANES, (j + 1) * LANES)
        stage[j] = jnp.where(upper, totals[:, cut], target[:, cut])

    def s_copy(r, source):
        peer = lax.rem(me + r, ndev)
        return pltpu.make_async_remote_copy(
            src_ref=stage.at[peer // (2 * nt)],
            dst_ref=stats.at[source],
            send_sem=s_send.at[r],
            recv_sem=s_recv.at[r],
            device_id=device(peer),
            device_id_type=MESH,
        )

    loop(1, ndev, lambda r: s_copy(r, me).start())
    stats[me] = stage[z]

    loop(1, nz, lambda r: z_copy(r, slot).wait_send())
    loop(0, nz, lambda r: sib_copy(r, z_source(r) + c).wait_send())
    loop(1, nt, lambda r: w_copy(r, t).wait_send())
    loop(1, nlines, lambda r: g_copy(r, slot, t).wait_send())

    def sent_gated(r):
        base, source_t = line_source(r)
        gs_copy(r, base + c, source_t).wait_send()

    loop(0, nlines, sent_gated)
    loop(1, ndev, lambda r: s_copy(r, lax.rem(me + ndev - r, ndev)).wait_recv())
    whole = jnp.sum(stats[...], axis=0)
    prop = whole[4:5, :] - jnp.log(whole[0:1, :])
    prop = jnp.where(c == 0, prop, pltpu.roll(prop, LANES - imps, 1))
    prop_out[...] = prop[:, :imps]
    loop(1, ndev, lambda r: s_copy(r, me).wait_send())


def local(events, lengths, packing, positions, logged, w_uvqk, w_out, catalogue):
    rows, width = events.shape
    imps = positions.shape[1]
    nz = lax.axis_size("item")
    nt = lax.axis_size("tensor")
    nslots = nz * 2
    ndev = nslots * nt
    items = catalogue.shape[0]
    total_imps = nslots * imps
    dma = pltpu.SemaphoreType.DMA
    smem = pl.BlockSpec(memory_space=pltpu.SMEM)
    vmem = pl.BlockSpec(memory_space=pltpu.VMEM)
    hbm = pl.BlockSpec(memory_space=pl.ANY)
    state, prop = pl.pallas_call(
        functools.partial(kernel, nz, nt),
        out_shape=(
            jax.ShapeDtypeStruct((imps, width // nt), jnp.bfloat16),
            jax.ShapeDtypeStruct((1, imps), jnp.float32),
        ),
        in_specs=[smem, smem, vmem, vmem, hbm, hbm, hbm, hbm],
        out_specs=(vmem, vmem),
        scratch_shapes=[
            pltpu.VMEM((rows, width), jnp.bfloat16),
            pltpu.VMEM((width, 2 * DH), jnp.bfloat16),
            pltpu.VMEM((width, 2 * DH), jnp.bfloat16),
            pltpu.VMEM((nt * DH, width), jnp.bfloat16),
            pltpu.VMEM((items, width), jnp.bfloat16),
            pltpu.VMEM((total_imps, width), jnp.bfloat16),
            pltpu.VMEM((total_imps, nt * DH), jnp.bfloat16),
            pltpu.VMEM((total_imps, width), jnp.bfloat16),
            pltpu.VMEM((1, total_imps), jnp.int32),
            pltpu.VMEM((nz, 8, LANES), jnp.float32),
            pltpu.VMEM((ndev, 8, LANES), jnp.float32),
            dma((7,)),
            dma((nz,)),
            dma((nz,)),
            dma((nz,)),
            dma((nz,)),
            dma((nz * nt,)),
            dma((nz * nt,)),
            dma((nz * nt,)),
            dma((nz * nt,)),
            dma((nt,)),
            dma((nt,)),
            dma((ndev,)),
            dma((ndev,)),
        ],
        compiler_params=pltpu.CompilerParams(
            collective_id=0, has_side_effects=True, vmem_limit_bytes=48 * 1024 * 1024
        ),
        name="replay",
    )(packing, lengths, positions, logged, events, w_uvqk, w_out, catalogue)
    return state, prop.reshape(imps)


def solution(mesh):
    placed = (
        P(("groups", "item", "dp"), None),
        P("groups"),
        P("groups"),
        P("groups", None),
        P("groups", None),
        P(None, "tensor"),
        P("tensor", None),
        P(("item", "dp", "tensor"), None),
    )
    return jax.shard_map(
        local,
        mesh=mesh,
        in_specs=placed,
        out_specs=(P(("groups", "item", "dp"), "tensor"), P(("groups", "item", "dp"))),
        check_vma=False,
    )
```

```python
import functools
import math

import jax
import jax.numpy as jnp
from jax import lax
from jax.experimental import pallas as pl
from jax.experimental.pallas import tpu as pltpu
from jax.sharding import PartitionSpec as P

DH = 128
LANES = 128
ITEM_BLOCK = 256
MESH = pl.DeviceIdType.MESH


def silu(x):
    return x / (1.0 + jnp.exp(-x))


def kernel(
    nz,
    nt,
    packing_hbm,
    lengths_hbm,
    positions_hbm,
    logged_hbm,
    events_hbm,
    w_hbm,
    w_out_hbm,
    cat_hbm,
    state_out,
    prop_out,
    packing,
    lengths,
    positions,
    logged,
    events,
    w_vk,
    w_uq,
    w_full,
    cat,
    chosen_all,
    gated_all,
    states,
    ids,
    stage,
    stats,
    load_sem,
    z_send,
    z_recv,
    x_send,
    x_recv,
    sib_send,
    sib_recv,
    w_send,
    w_recv,
    ws_send,
    ws_recv,
    g_send,
    g_recv,
    gs_send,
    gs_recv,
    s_send,
    s_recv,
):
    z = lax.axis_index("item")
    c = lax.axis_index("dp")
    t = lax.axis_index("tensor")
    slot = z * 2 + c
    other = 1 - c
    imps = positions.shape[1]
    rows, width = events.shape
    share = width // nt
    nslots = nz * 2
    nlines = nz * nt
    ndev = nlines * 2
    me = slot * nt + t

    def each_z(first, body):
        if nz <= 4:
            for r in range(first, nz):
                body(r)
        else:
            lax.fori_loop(first, nz, lambda r, carry: (body(r), carry)[1], 0)

    def z_at(r):
        return lax.rem(z + r, nz)

    def z_from(r):
        return lax.rem(z + nz - r, nz)

    def t_at(r):
        return lax.rem(t + r, nt)

    def t_from(r):
        return lax.rem(t + nt - r, nt)

    def each_peer(body):
        for dt in range(nt):
            for dc in range(2):
                each_z(
                    0 if dt or dc else 1,
                    lambda r: body(z_at(r), other if dc else c, t_at(dt)),
                )

    def each_line(body):
        for dt in range(nt):
            each_z(0 if dt else 1, lambda r: body(r, dt))

    def remote(src, dst, send_sem, recv_sem, **device_id):
        return pltpu.make_async_remote_copy(
            src_ref=src,
            dst_ref=dst,
            send_sem=send_sem,
            recv_sem=recv_sem,
            device_id=device_id,
            device_id_type=MESH,
        )

    loads = [
        pltpu.make_async_copy(events_hbm, events, load_sem.at[0]),
        pltpu.make_async_copy(w_hbm.at[:, 0:DH], w_uq.at[:, 0:DH], load_sem.at[1]),
        pltpu.make_async_copy(w_hbm.at[:, 2 * DH : 3 * DH], w_uq.at[:, DH : 2 * DH], load_sem.at[2]),
        pltpu.make_async_copy(w_hbm.at[:, DH : 2 * DH], w_vk.at[:, 0:DH], load_sem.at[3]),
        pltpu.make_async_copy(w_hbm.at[:, 3 * DH : 4 * DH], w_vk.at[:, DH : 2 * DH], load_sem.at[4]),
        pltpu.make_async_copy(w_out_hbm, w_full.at[pl.ds(pl.multiple_of(t * DH, DH), DH), :], load_sem.at[5]),
        pltpu.make_async_copy(cat_hbm, cat, load_sem.at[6]),
    ]
    small = [
        pltpu.make_async_copy(packing_hbm, packing, load_sem.at[7]),
        pltpu.make_async_copy(lengths_hbm, lengths, load_sem.at[8]),
        pltpu.make_async_copy(positions_hbm, positions, load_sem.at[9]),
        pltpu.make_async_copy(logged_hbm, logged, load_sem.at[10]),
    ]
    for copy in small:
        copy.start()
    for copy in loads:
        copy.start()

    barrier = pltpu.get_barrier_semaphore()

    def greet(peer_z, peer_c, peer_t):
        peer = {"item": peer_z, "dp": peer_c, "tensor": peer_t}
        pl.semaphore_signal(barrier, inc=1, device_id=peer, device_id_type=MESH)

    each_peer(greet)

    for copy in small:
        copy.wait()
    hist = packing[slot]
    length = lengths[hist].astype(jnp.float32)
    pos_row = positions[pl.ds(hist, 1), :].astype(jnp.float32)
    eye = lax.broadcasted_iota(jnp.int32, (imps, imps), 0) == lax.broadcasted_iota(
        jnp.int32, (imps, imps), 1
    )
    pos_col = jnp.sum(jnp.where(eye, pos_row, 0.0), axis=1, keepdims=True)
    spots = lax.broadcasted_iota(jnp.int32, (imps, rows), 1).astype(jnp.float32)
    pick = jnp.where(spots == pos_col, 1.0, 0.0).astype(jnp.bfloat16)
    for j in range(nslots):
        ids[0:1, j * imps : (j + 1) * imps] = logged[pl.ds(packing[j], 1), :]

    def rows_of(which):
        return pl.ds(pl.multiple_of(which * imps, imps), imps)

    loads[0].wait()
    chosen = jnp.dot(pick, events[...], preferred_element_type=jnp.float32).astype(jnp.bfloat16)
    chosen_all[rows_of(slot), :] = chosen
    pl.semaphore_wait(barrier, ndev - 1)

    def cols_of(which):
        return pl.ds(pl.multiple_of(which * share, LANES), share)

    def head_cols(which):
        return pl.ds(pl.multiple_of(which * DH, DH), DH)

    def z_copy(r, source_z):
        part = chosen_all.at[rows_of(source_z * 2 + c), cols_of(t)]
        return remote(part, part, z_send.at[r], z_recv.at[r], item=z_at(r))

    def x_copy(r, dt, source_t):
        part = chosen_all.at[rows_of(z_from(r) * 2 + c), cols_of(source_t)]
        k = r * nt + dt
        return remote(part, part, x_send.at[k], x_recv.at[k], tensor=t_at(dt))

    def sib_copy(r, source_c):
        part = chosen_all.at[rows_of(z_from(r) * 2 + source_c), :]
        return remote(part, part, sib_send.at[r], sib_recv.at[r], dp=other)

    half = DH // 2

    def w_rows(source_t, source_c):
        return w_full.at[pl.ds(pl.multiple_of(source_t * DH + source_c * half, half), half), :]

    def w_copy(dt, source_t):
        part = w_out_hbm.at[pl.ds(pl.multiple_of(c * half, half), half), :]
        return remote(
            part, w_rows(source_t, c), w_send.at[dt], w_recv.at[dt], tensor=t_at(dt)
        )

    def ws_copy(dt, source_c):
        part = w_rows(t_from(dt), source_c)
        return remote(part, part, ws_send.at[dt], ws_recv.at[dt], dp=other)

    def gated_at(source_z, source_c, source_t):
        return gated_all.at[rows_of(source_z * 2 + source_c), head_cols(source_t)]

    def g_copy(r, dt, source_z, source_t):
        part = gated_at(source_z, c, source_t)
        k = r * nt + dt
        return remote(part, part, g_send.at[k], g_recv.at[k], item=z_at(r), tensor=t_at(dt))

    def gs_copy(r, dt):
        part = gated_at(z_from(r), c, t_from(dt))
        return remote(part, part, gs_send.at[r * nt + dt], gs_recv, dp=other)

    each_z(1, lambda r: z_copy(r, z).start())
    for dt in range(1, nt):
        w_copy(dt, t).start()
    sib_copy(0, c).start()

    loads[1].wait()
    loads[2].wait()
    gate_query = silu(
        jnp.dot(chosen, w_uq[...], preferred_element_type=jnp.float32)
    ).astype(jnp.bfloat16)
    loads[3].wait()
    loads[4].wait()
    values_keys = silu(
        jnp.dot(events[...], w_vk[...], preferred_element_type=jnp.float32)
    ).astype(jnp.bfloat16)
    scores = lax.dot_general(
        gate_query[:, DH:],
        values_keys[:, DH:],
        (((1,), (1,)), ((), ())),
        preferred_element_type=jnp.float32,
    ) * (1.0 / math.sqrt(DH))
    is_valid = (spots <= pos_col) & (spots < length)
    weights = jnp.where(is_valid, silu(scores), 0.0).astype(jnp.bfloat16)
    attended = jnp.dot(weights, values_keys[:, :DH], preferred_element_type=jnp.float32)
    inverse = lax.rsqrt(jnp.mean(attended * attended, axis=-1, keepdims=True) + 1e-06)
    gated = (attended * inverse * gate_query[:, :DH].astype(jnp.float32)).astype(jnp.bfloat16)
    gated_all[rows_of(slot), head_cols(t)] = gated

    each_line(lambda r, dt: g_copy(r, dt, z, t).start())
    gs_copy(0, 0).start()
    for dt in range(1, nt):
        w_copy(dt, t_from(dt)).wait_recv()
        ws_copy(dt, c).start()

    def pass_across(r):
        z_copy(r, z_from(r)).wait_recv()
        for dt in range(1, nt):
            x_copy(r, dt, t).start()

    each_z(1, pass_across)

    def pass_gated(r, dt):
        g_copy(r, dt, z_from(r), t_from(dt)).wait_recv()
        gs_copy(r, dt).start()

    each_line(pass_gated)

    def pass_chosen(r):
        for dt in range(1, nt):
            x_copy(r, dt, t_from(dt)).wait_recv()
        sib_copy(r, c).start()

    each_z(1, pass_chosen)

    loads[5].wait()
    loads[6].wait()
    for dt in range(1, nt):
        ws_copy(dt, other).wait_recv()
    arrived = gated_all.at[0 : nz * imps, :]
    remote(arrived, arrived, gs_send.at[0], gs_recv, dp=other).wait_recv()
    each_z(0, lambda r: sib_copy(r, other).wait_recv())

    states[...] = (
        jnp.dot(gated_all[...], w_full[...], preferred_element_type=jnp.float32)
        + chosen_all[...].astype(jnp.float32)
    ).astype(jnp.bfloat16)
    state_out[...] = states[rows_of(slot), cols_of(t)]

    items = cat.shape[0]
    item_ids = ids[...]

    def block(b, carry):
        totals, target = carry
        logits = lax.dot_general(
            cat[pl.ds(pl.multiple_of(b * ITEM_BLOCK, ITEM_BLOCK), ITEM_BLOCK), :],
            states[...],
            (((1,), (1,)), ((), ())),
            preferred_element_type=jnp.float32,
        )
        local = item_ids - (me * items + b * ITEM_BLOCK)
        matches = lax.broadcasted_iota(jnp.int32, logits.shape, 0) == local
        totals = totals + jnp.sum(jnp.exp(logits), axis=0, keepdims=True)
        target = target + jnp.sum(jnp.where(matches, logits, 0.0), axis=0, keepdims=True)
        return totals, target

    zero = jnp.zeros((1, nslots * imps), jnp.float32)
    totals, target = lax.fori_loop(0, items // ITEM_BLOCK, block, (zero, zero))
    upper = lax.broadcasted_iota(jnp.int32, (8, LANES), 0) < 4
    for j in range(nz):
        cut = slice(j * LANES, (j + 1) * LANES)
        stage[j] = jnp.where(upper, totals[:, cut], target[:, cut])

    def s_copy(peer_z, peer_c, peer_t):
        remote(
            stage.at[peer_z], stats.at[me], s_send, s_recv, item=peer_z, dp=peer_c, tensor=peer_t
        ).start()

    each_peer(s_copy)
    stats[me] = stage[z]

    each_z(1, lambda r: z_copy(r, z).wait_send())
    each_z(0, lambda r: sib_copy(r, c).wait_send())
    for dt in range(1, nt):
        w_copy(dt, t).wait_send()
        ws_copy(dt, c).wait_send()
        each_z(1, lambda r: x_copy(r, dt, t).wait_send())
    each_line(lambda r, dt: g_copy(r, dt, z, t).wait_send())
    each_z(0, lambda r: [gs_copy(r, dt).wait_send() for dt in range(nt)])
    others = stats.at[0 : ndev - 1]
    all_stats = remote(others, others, s_send, s_recv, dp=other)
    all_stats.wait_recv()
    whole = jnp.sum(stats[...], axis=0)
    prop = whole[4:5, :] - jnp.log(whole[0:1, :])
    prop = jnp.where(c == 0, prop, pltpu.roll(prop, LANES - imps, 1))
    prop_out[...] = prop[:, :imps]
    all_stats.wait_send()


def local(events, lengths, packing, positions, logged, w_uvqk, w_out, catalogue):
    rows, width = events.shape
    imps = positions.shape[1]
    nz = lax.axis_size("item")
    nt = lax.axis_size("tensor")
    nslots = nz * 2
    ndev = nslots * nt
    items = catalogue.shape[0]
    total_imps = nslots * imps
    dma = pltpu.SemaphoreType.DMA
    vmem = pl.BlockSpec(memory_space=pltpu.VMEM)
    hbm = pl.BlockSpec(memory_space=pltpu.HBM)
    state, prop = pl.pallas_call(
        functools.partial(kernel, nz, nt),
        out_shape=(
            jax.ShapeDtypeStruct((imps, width // nt), jnp.bfloat16),
            jax.ShapeDtypeStruct((1, imps), jnp.float32),
        ),
        in_specs=[hbm] * 8,
        out_specs=(vmem, vmem),
        scratch_shapes=[
            pltpu.SMEM(packing.shape, jnp.int32),
            pltpu.SMEM(lengths.shape, jnp.int32),
            pltpu.VMEM(positions.shape, jnp.int32),
            pltpu.VMEM(logged.shape, jnp.int32),
            pltpu.VMEM((rows, width), jnp.bfloat16),
            pltpu.VMEM((width, 2 * DH), jnp.bfloat16),
            pltpu.VMEM((width, 2 * DH), jnp.bfloat16),
            pltpu.VMEM((nt * DH, width), jnp.bfloat16),
            pltpu.VMEM((items, width), jnp.bfloat16),
            pltpu.VMEM((total_imps, width), jnp.bfloat16),
            pltpu.VMEM((total_imps, nt * DH), jnp.bfloat16),
            pltpu.VMEM((total_imps, width), jnp.bfloat16),
            pltpu.VMEM((1, total_imps), jnp.int32),
            pltpu.VMEM((nz, 8, LANES), jnp.float32),
            pltpu.VMEM((ndev, 8, LANES), jnp.float32),
            dma((11,)),
            dma((nz,)),
            dma((nz,)),
            dma((nz * nt,)),
            dma((nz * nt,)),
            dma((nz,)),
            dma((nz,)),
            dma((nt,)),
            dma((nt,)),
            dma((nt,)),
            dma((nt,)),
            dma((nz * nt,)),
            dma((nz * nt,)),
            dma((nz * nt,)),
            dma,
            dma,
            dma,
        ],
        compiler_params=pltpu.CompilerParams(
            collective_id=0, has_side_effects=True, vmem_limit_bytes=63 * 1024 * 1024
        ),
        name="replay",
    )(packing, lengths, positions, logged, events, w_uvqk, w_out, catalogue)
    return state, prop.reshape(imps)


def solution(mesh):
    placed = (
        P(("groups", "item", "dp"), None),
        P("groups"),
        P("groups"),
        P("groups", None),
        P("groups", None),
        P(None, "tensor"),
        P("tensor", None),
        P(("item", "dp", "tensor"), None),
    )
    return jax.shard_map(
        local,
        mesh=mesh,
        in_specs=placed,
        out_specs=(P(("groups", "item", "dp"), "tensor"), P(("groups", "item", "dp"))),
        check_vma=False,
    )
```

```python
import functools
import math

import jax
import jax.numpy as jnp
from jax import lax
from jax.experimental import pallas as pl
from jax.experimental.pallas import tpu as pltpu
from jax.sharding import PartitionSpec as P

DH = 128
LANES = 128
ITEM_BLOCK = 256
MESH = pl.DeviceIdType.MESH


def silu(x):
    return x / (1.0 + jnp.exp(-x))


def kernel(
    nz,
    nt,
    packing_hbm,
    lengths_hbm,
    positions_hbm,
    logged_hbm,
    events_hbm,
    w_hbm,
    w_out_hbm,
    cat_hbm,
    state_out,
    prop_out,
    packing,
    lengths,
    positions,
    logged,
    events,
    w_vk,
    w_uq,
    w_full,
    cat,
    chosen_all,
    gated_all,
    states,
    ids,
    stage,
    stats,
    load_sem,
    z_send,
    z_recv,
    x_send,
    x_recv,
    w_send,
    w_recv,
    ws_send,
    ws_recv,
    g_send,
    g_recv,
    c_send,
    c_recv,
    s_send,
    s_recv,
):
    z = lax.axis_index("item")
    c = lax.axis_index("dp")
    t = lax.axis_index("tensor")
    slot = z * 2 + c
    other = 1 - c
    imps = positions.shape[1]
    rows, width = events.shape
    share = width // nt
    nlines = nz * nt
    line = z * nt + t

    def each_z(first, body, last=nz):
        if nz <= 4:
            for r in range(first, last):
                body(r)
        else:
            lax.fori_loop(first, last, lambda r, carry: (body(r), carry)[1], 0)

    def z_at(r):
        return lax.rem(z + r, nz)

    def z_from(r):
        return lax.rem(z + nz - r, nz)

    def t_at(r):
        return lax.rem(t + r, nt)

    def t_from(r):
        return lax.rem(t + nt - r, nt)

    def each_line(body):
        for dt in range(nt):
            each_z(0 if dt else 1, lambda r: body(r, dt))

    def remote(src, dst, send_sem, recv_sem, **device_id):
        return pltpu.make_async_remote_copy(
            src_ref=src,
            dst_ref=dst,
            send_sem=send_sem,
            recv_sem=recv_sem,
            device_id=device_id,
            device_id_type=MESH,
        )

    loads = [
        pltpu.make_async_copy(events_hbm, events, load_sem.at[0]),
        pltpu.make_async_copy(w_hbm.at[:, 0:DH], w_uq.at[:, 0:DH], load_sem.at[1]),
        pltpu.make_async_copy(w_hbm.at[:, 2 * DH : 3 * DH], w_uq.at[:, DH : 2 * DH], load_sem.at[2]),
        pltpu.make_async_copy(w_hbm.at[:, DH : 2 * DH], w_vk.at[:, 0:DH], load_sem.at[3]),
        pltpu.make_async_copy(w_hbm.at[:, 3 * DH : 4 * DH], w_vk.at[:, DH : 2 * DH], load_sem.at[4]),
        pltpu.make_async_copy(w_out_hbm, w_full.at[pl.ds(pl.multiple_of(t * DH, DH), DH), :], load_sem.at[5]),
        pltpu.make_async_copy(cat_hbm, cat.at[0], load_sem.at[6]),
    ]
    small = [
        pltpu.make_async_copy(packing_hbm, packing, load_sem.at[7]),
        pltpu.make_async_copy(lengths_hbm, lengths, load_sem.at[8]),
        pltpu.make_async_copy(positions_hbm, positions, load_sem.at[9]),
        pltpu.make_async_copy(logged_hbm, logged, load_sem.at[10]),
    ]
    for copy in small:
        copy.start()
    for copy in loads:
        copy.start()

    barrier = pltpu.get_barrier_semaphore()

    def greet(**peer):
        pl.semaphore_signal(barrier, inc=1, device_id=peer, device_id_type=MESH)

    greet(dp=other)
    each_line(lambda r, dt: greet(item=z_at(r), tensor=t_at(dt)))

    for copy in small:
        copy.wait()
    hist = packing[slot]
    length = lengths[hist].astype(jnp.float32)
    pos_row = positions[pl.ds(hist, 1), :].astype(jnp.float32)
    eye = lax.broadcasted_iota(jnp.int32, (imps, imps), 0) == lax.broadcasted_iota(
        jnp.int32, (imps, imps), 1
    )
    pos_col = jnp.sum(jnp.where(eye, pos_row, 0.0), axis=1, keepdims=True)
    spots = lax.broadcasted_iota(jnp.int32, (imps, rows), 1).astype(jnp.float32)
    pick = jnp.where(spots == pos_col, 1.0, 0.0).astype(jnp.bfloat16)
    for r in range(nz):
        ids[0:1, r * imps : (r + 1) * imps] = logged[pl.ds(packing[z_from(r) * 2 + c], 1), :]

    def rows_of(r):
        return pl.ds(r * imps, imps)

    loads[0].wait()
    chosen = jnp.dot(pick, events[...], preferred_element_type=jnp.float32).astype(jnp.bfloat16)
    chosen_all[rows_of(0), :] = chosen

    def cols_of(which):
        return pl.ds(pl.multiple_of(which * share, LANES), share)

    def head_cols(which):
        return pl.ds(pl.multiple_of(which * DH, DH), DH)

    def z_copy(r):
        return remote(
            chosen_all.at[rows_of(0), cols_of(t)],
            chosen_all.at[rows_of(r), cols_of(t)],
            z_send.at[r],
            z_recv.at[r],
            item=z_at(r),
        )

    def x_copy(r, dt, source_t):
        part = chosen_all.at[rows_of(r), cols_of(source_t)]
        k = r * nt + dt
        return remote(part, part, x_send.at[k], x_recv.at[k], tensor=t_at(dt))

    def cat_copy():
        return remote(cat_hbm, cat.at[1], c_send, c_recv, dp=other)

    half = DH // 2

    def w_rows(source_t, source_c):
        return w_full.at[pl.ds(pl.multiple_of(source_t * DH + source_c * half, half), half), :]

    def w_copy(dt, source_t):
        part = w_out_hbm.at[pl.ds(pl.multiple_of(c * half, half), half), :]
        return remote(
            part, w_rows(source_t, c), w_send.at[dt], w_recv.at[dt], tensor=t_at(dt)
        )

    def ws_copy(dt, source_c):
        part = w_rows(t_from(dt), source_c)
        return remote(part, part, ws_send.at[dt], ws_recv.at[dt], dp=other)

    def gated_at(r, source_t):
        return gated_all.at[rows_of(r), head_cols(source_t)]

    def g_copy(r, dt, source_t):
        k = r * nt + dt
        return remote(
            gated_at(0, source_t),
            gated_at(r, source_t),
            g_send.at[k],
            g_recv.at[k],
            item=z_at(r),
            tensor=t_at(dt),
        )

    pl.semaphore_wait(barrier, nlines)
    each_z(1, lambda r: z_copy(r).start())
    for dt in range(1, nt):
        w_copy(dt, t).start()
    cat_copy().start()
    loads[1].wait()
    loads[2].wait()
    gate_query = silu(
        jnp.dot(chosen, w_uq[...], preferred_element_type=jnp.float32)
    ).astype(jnp.bfloat16)
    loads[3].wait()
    loads[4].wait()
    values_keys = silu(
        jnp.dot(events[...], w_vk[...], preferred_element_type=jnp.float32)
    ).astype(jnp.bfloat16)
    scores = lax.dot_general(
        gate_query[:, DH:],
        values_keys[:, DH:],
        (((1,), (1,)), ((), ())),
        preferred_element_type=jnp.float32,
    ) * (1.0 / math.sqrt(DH))
    is_valid = (spots <= pos_col) & (spots < length)
    weights = jnp.where(is_valid, silu(scores), 0.0).astype(jnp.bfloat16)
    attended = jnp.dot(weights, values_keys[:, :DH], preferred_element_type=jnp.float32)
    inverse = lax.rsqrt(jnp.mean(attended * attended, axis=-1, keepdims=True) + 1e-06)
    gated = (attended * inverse * gate_query[:, :DH].astype(jnp.float32)).astype(jnp.bfloat16)

    gated_all[rows_of(0), head_cols(t)] = gated
    each_line(lambda r, dt: g_copy(r, dt, t).start())

    def pass_across(r):
        z_copy(r).wait_recv()
        for dt in range(1, nt):
            x_copy(r, dt, t).start()

    each_z(1, pass_across)
    for dt in range(1, nt):
        w_copy(dt, t_from(dt)).wait_recv()
        ws_copy(dt, c).start()

    each_line(lambda r, dt: g_copy(r, dt, t_from(dt)).wait_recv())
    for dt in range(1, nt):
        ws_copy(dt, other).wait_recv()
    loads[5].wait()

    def take_across(r):
        for dt in range(1, nt):
            x_copy(r, dt, t_from(dt)).wait_recv()

    each_z(1, take_across)
    states[...] = (
        jnp.dot(gated_all[...], w_full[...], preferred_element_type=jnp.float32)
        + chosen_all[...].astype(jnp.float32)
    ).astype(jnp.bfloat16)
    state_out[...] = states[rows_of(0), cols_of(t)]

    items = cat.shape[1]
    item_ids = ids[...]

    def score(shard, source_c, carry):
        base = ((z * 2 + source_c) * nt + t) * items

        def block(b, carry):
            totals, target = carry
            logits = lax.dot_general(
                cat[shard, pl.ds(pl.multiple_of(b * ITEM_BLOCK, ITEM_BLOCK), ITEM_BLOCK), :],
                states[...],
                (((1,), (1,)), ((), ())),
                preferred_element_type=jnp.float32,
            )
            local = item_ids - (base + b * ITEM_BLOCK)
            matches = lax.broadcasted_iota(jnp.int32, logits.shape, 0) == local
            totals = totals + jnp.sum(jnp.exp(logits), axis=0, keepdims=True)
            target = target + jnp.sum(jnp.where(matches, logits, 0.0), axis=0, keepdims=True)
            return totals, target

        return lax.fori_loop(0, items // ITEM_BLOCK, block, carry)

    zero = jnp.zeros((1, nz * imps), jnp.float32)
    loads[6].wait()
    carry = score(0, c, (zero, zero))
    cat_copy().wait_recv()
    totals, target = score(1, other, carry)
    upper = lax.broadcasted_iota(jnp.int32, (8, LANES), 0) < 4
    for r in range(nz):
        cut = slice(r // 2 * LANES, (r // 2 + 1) * LANES)
        tile = jnp.where(upper, totals[:, cut], target[:, cut])
        stage[r] = pltpu.roll(tile, LANES - imps, 1) if r % 2 else tile

    def s_copy(r, dt):
        remote(
            stage.at[r], stats.at[line], s_send, s_recv, item=z_from(r), tensor=t_at(dt)
        ).start()

    each_line(s_copy)
    stats[line] = stage[0]

    each_z(1, lambda r: z_copy(r).wait_send())
    cat_copy().wait_send()
    for dt in range(1, nt):
        w_copy(dt, t).wait_send()
        ws_copy(dt, c).wait_send()
        each_z(1, lambda r: x_copy(r, dt, t).wait_send())
    each_line(lambda r, dt: g_copy(r, dt, t).wait_send())
    others = stats.at[0 : nlines - 1]
    all_stats = remote(others, others, s_send, s_recv, dp=other)
    all_stats.wait_recv()
    whole = jnp.sum(stats[...], axis=0)
    prop = whole[4:5, :] - jnp.log(whole[0:1, :])
    prop_out[...] = prop[:, :imps]
    all_stats.wait_send()


def local(events, lengths, packing, positions, logged, w_uvqk, w_out, catalogue):
    rows, width = events.shape
    imps = positions.shape[1]
    nz = lax.axis_size("item")
    nt = lax.axis_size("tensor")
    items = catalogue.shape[0]
    dma = pltpu.SemaphoreType.DMA
    vmem = pl.BlockSpec(memory_space=pltpu.VMEM)
    hbm = pl.BlockSpec(memory_space=pltpu.HBM)
    state, prop = pl.pallas_call(
        functools.partial(kernel, nz, nt),
        out_shape=(
            jax.ShapeDtypeStruct((imps, width // nt), jnp.bfloat16),
            jax.ShapeDtypeStruct((1, imps), jnp.float32),
        ),
        in_specs=[hbm] * 8,
        out_specs=(vmem, vmem),
        scratch_shapes=[
            pltpu.SMEM(packing.shape, jnp.int32),
            pltpu.SMEM(lengths.shape, jnp.int32),
            pltpu.VMEM(positions.shape, jnp.int32),
            pltpu.VMEM(logged.shape, jnp.int32),
            pltpu.VMEM((rows, width), jnp.bfloat16),
            pltpu.VMEM((width, 2 * DH), jnp.bfloat16),
            pltpu.VMEM((width, 2 * DH), jnp.bfloat16),
            pltpu.VMEM((nt * DH, width), jnp.bfloat16),
            pltpu.VMEM((2, items, width), jnp.bfloat16),
            pltpu.VMEM((nz * imps, width), jnp.bfloat16),
            pltpu.VMEM((nz * imps, nt * DH), jnp.bfloat16),
            pltpu.VMEM((nz * imps, width), jnp.bfloat16),
            pltpu.VMEM((1, nz * imps), jnp.int32),
            pltpu.VMEM((nz, 8, LANES), jnp.float32),
            pltpu.VMEM((nz * nt, 8, LANES), jnp.float32),
            dma((11,)),
            dma((nz,)),
            dma((nz,)),
            dma((nz * nt,)),
            dma((nz * nt,)),
            dma((nt,)),
            dma((nt,)),
            dma((nt,)),
            dma((nt,)),
            dma((nz * nt,)),
            dma((nz * nt,)),
            dma,
            dma,
            dma,
            dma,
        ],
        compiler_params=pltpu.CompilerParams(
            collective_id=0, has_side_effects=True, vmem_limit_bytes=63 * 1024 * 1024
        ),
        name="replay",
    )(packing, lengths, positions, logged, events, w_uvqk, w_out, catalogue)
    return state, prop.reshape(imps)


def solution(mesh):
    placed = (
        P(("groups", "item", "dp"), None),
        P("groups"),
        P("groups"),
        P("groups", None),
        P("groups", None),
        P(None, "tensor"),
        P("tensor", None),
        P(("item", "dp", "tensor"), None),
    )
    return jax.shard_map(
        local,
        mesh=mesh,
        in_specs=placed,
        out_specs=(P(("groups", "item", "dp"), "tensor"), P(("groups", "item", "dp"))),
        check_vma=False,
    )
```

```python
import functools
import math

import jax
import jax.numpy as jnp
from jax import lax
from jax.experimental import pallas as pl
from jax.experimental.pallas import tpu as pltpu
from jax.sharding import PartitionSpec as P

DH = 128
LANES = 128
ITEM_BLOCK = 512
MESH = pl.DeviceIdType.MESH


def silu(x):
    return x / (1.0 + jnp.exp(-x))


def kernel(
    nz,
    nt,
    packing_hbm,
    lengths_hbm,
    positions_hbm,
    logged_hbm,
    events_hbm,
    w_hbm,
    w_out_hbm,
    cat_hbm,
    state_out,
    prop_out,
    packing,
    lengths,
    positions,
    logged,
    events,
    w_vk,
    w_uq,
    w_full,
    cat,
    chosen_all,
    gated_all,
    states,
    ids,
    stage,
    stats,
    load_sem,
    z_send,
    z_recv,
    x_send,
    x_recv,
    w_send,
    w_recv,
    ws_send,
    ws_recv,
    g_send,
    g_recv,
    c_send,
    c_recv,
    s_send,
    s_recv,
):
    z = lax.axis_index("item")
    c = lax.axis_index("dp")
    t = lax.axis_index("tensor")
    slot = z * 2 + c
    other = 1 - c
    imps = positions.shape[1]
    rows, width = events.shape
    share = width // nt
    nlines = nz * nt
    line = z * nt + t

    def each_z(first, body, last=nz):
        if nz <= 4:
            for r in range(first, last):
                body(r)
        else:
            lax.fori_loop(first, last, lambda r, carry: (body(r), carry)[1], 0)

    def z_at(r):
        return lax.rem(z + r, nz)

    def z_from(r):
        return lax.rem(z + nz - r, nz)

    def t_at(r):
        return lax.rem(t + r, nt)

    def t_from(r):
        return lax.rem(t + nt - r, nt)

    def each_line(body):
        for dt in range(nt):
            each_z(0 if dt else 1, lambda r: body(r, dt))

    def remote(src, dst, send_sem, recv_sem, **device_id):
        return pltpu.make_async_remote_copy(
            src_ref=src,
            dst_ref=dst,
            send_sem=send_sem,
            recv_sem=recv_sem,
            device_id=device_id,
            device_id_type=MESH,
        )

    loads = [
        pltpu.make_async_copy(events_hbm, events, load_sem.at[0]),
        pltpu.make_async_copy(w_hbm.at[:, 0:DH], w_uq.at[:, 0:DH], load_sem.at[1]),
        pltpu.make_async_copy(w_hbm.at[:, 2 * DH : 3 * DH], w_uq.at[:, DH : 2 * DH], load_sem.at[2]),
        pltpu.make_async_copy(w_hbm.at[:, DH : 2 * DH], w_vk.at[:, 0:DH], load_sem.at[3]),
        pltpu.make_async_copy(w_hbm.at[:, 3 * DH : 4 * DH], w_vk.at[:, DH : 2 * DH], load_sem.at[4]),
        pltpu.make_async_copy(w_out_hbm, w_full.at[pl.ds(pl.multiple_of(t * DH, DH), DH), :], load_sem.at[5]),
        pltpu.make_async_copy(cat_hbm, cat.at[0], load_sem.at[6]),
    ]
    small = [
        pltpu.make_async_copy(packing_hbm, packing, load_sem.at[7]),
        pltpu.make_async_copy(lengths_hbm, lengths, load_sem.at[8]),
        pltpu.make_async_copy(positions_hbm, positions, load_sem.at[9]),
        pltpu.make_async_copy(logged_hbm, logged, load_sem.at[10]),
    ]
    for copy in small:
        copy.start()
    loads[0].start()

    barrier = pltpu.get_barrier_semaphore()

    def greet(**peer):
        pl.semaphore_signal(barrier, inc=1, device_id=peer, device_id_type=MESH)

    greet(dp=other)
    each_line(lambda r, dt: greet(item=z_at(r), tensor=t_at(dt)))

    for copy in small:
        copy.wait()
    hist = packing[slot]
    length = lengths[hist].astype(jnp.float32)
    pos_row = positions[pl.ds(hist, 1), :].astype(jnp.float32)
    eye = lax.broadcasted_iota(jnp.int32, (imps, imps), 0) == lax.broadcasted_iota(
        jnp.int32, (imps, imps), 1
    )
    pos_col = jnp.sum(jnp.where(eye, pos_row, 0.0), axis=1, keepdims=True)
    spots = lax.broadcasted_iota(jnp.int32, (imps, rows), 1).astype(jnp.float32)
    pick = jnp.where(spots == pos_col, 1.0, 0.0).astype(jnp.bfloat16)
    for r in range(nz):
        ids[0:1, r * imps : (r + 1) * imps] = logged[pl.ds(packing[z_from(r) * 2 + c], 1), :]

    def rows_of(r):
        return pl.ds(r * imps, imps)

    loads[0].wait()
    for copy in loads[1:]:
        copy.start()
    chosen = jnp.dot(pick, events[...], preferred_element_type=jnp.float32).astype(jnp.bfloat16)
    chosen_all[rows_of(0), :] = chosen

    def cols_of(which):
        return pl.ds(pl.multiple_of(which * share, LANES), share)

    def head_cols(which):
        return pl.ds(pl.multiple_of(which * DH, DH), DH)

    def z_copy(r):
        return remote(
            chosen_all.at[rows_of(0), cols_of(t)],
            chosen_all.at[rows_of(r), cols_of(t)],
            z_send.at[r],
            z_recv.at[r],
            item=z_at(r),
        )

    def x_copy(r, dt, source_t):
        part = chosen_all.at[rows_of(r), cols_of(source_t)]
        k = r * nt + dt
        return remote(part, part, x_send.at[k], x_recv.at[k], tensor=t_at(dt))

    def cat_copy():
        return remote(cat_hbm, cat.at[1], c_send, c_recv, dp=other)

    half = DH // 2

    def w_rows(source_t, source_c):
        return w_full.at[pl.ds(pl.multiple_of(source_t * DH + source_c * half, half), half), :]

    def w_copy(dt, source_t):
        part = w_out_hbm.at[pl.ds(pl.multiple_of(c * half, half), half), :]
        return remote(
            part, w_rows(source_t, c), w_send.at[dt], w_recv.at[dt], tensor=t_at(dt)
        )

    def ws_copy(dt, source_c):
        part = w_rows(t_from(dt), source_c)
        return remote(part, part, ws_send.at[dt], ws_recv.at[dt], dp=other)

    def gated_at(r, source_t):
        return gated_all.at[rows_of(r), head_cols(source_t)]

    def g_copy(r, dt, source_t):
        k = r * nt + dt
        return remote(
            gated_at(0, source_t),
            gated_at(r, source_t),
            g_send.at[k],
            g_recv.at[k],
            item=z_at(r),
            tensor=t_at(dt),
        )

    pl.semaphore_wait(barrier, nlines)
    each_z(1, lambda r: z_copy(r).start())
    for dt in range(1, nt):
        w_copy(dt, t).start()
    cat_copy().start()
    loads[1].wait()
    loads[2].wait()
    gate_query = silu(
        jnp.dot(chosen, w_uq[...], preferred_element_type=jnp.float32)
    ).astype(jnp.bfloat16)
    loads[3].wait()
    loads[4].wait()
    values_keys = silu(
        jnp.dot(events[...], w_vk[...], preferred_element_type=jnp.float32)
    ).astype(jnp.bfloat16)
    def pass_across(r):
        z_copy(r).wait_recv()
        for dt in range(1, nt):
            x_copy(r, dt, t).start()

    each_z(1, pass_across)
    scores = lax.dot_general(
        gate_query[:, DH:],
        values_keys[:, DH:],
        (((1,), (1,)), ((), ())),
        preferred_element_type=jnp.float32,
    ) * (1.0 / math.sqrt(DH))
    is_valid = (spots <= pos_col) & (spots < length)
    weights = jnp.where(is_valid, silu(scores), 0.0).astype(jnp.bfloat16)
    attended = jnp.dot(weights, values_keys[:, :DH], preferred_element_type=jnp.float32)
    inverse = lax.rsqrt(jnp.mean(attended * attended, axis=-1, keepdims=True) + 1e-06)
    gated = (attended * inverse * gate_query[:, :DH].astype(jnp.float32)).astype(jnp.bfloat16)

    gated_all[rows_of(0), head_cols(t)] = gated
    each_line(lambda r, dt: g_copy(r, dt, t).start())

    for dt in range(1, nt):
        w_copy(dt, t_from(dt)).wait_recv()
        ws_copy(dt, c).start()

    each_line(lambda r, dt: g_copy(r, dt, t_from(dt)).wait_recv())
    for dt in range(1, nt):
        ws_copy(dt, other).wait_recv()
    loads[5].wait()

    def take_across(r):
        for dt in range(1, nt):
            x_copy(r, dt, t_from(dt)).wait_recv()

    each_z(1, take_across)
    states[...] = (
        jnp.dot(gated_all[...], w_full[...], preferred_element_type=jnp.float32)
        + chosen_all[...].astype(jnp.float32)
    ).astype(jnp.bfloat16)
    state_out[...] = states[rows_of(0), cols_of(t)]

    items = cat.shape[1]
    item_ids = ids[...]

    def score(shard, source_c, carry):
        base = ((z * 2 + source_c) * nt + t) * items

        def block(b, carry):
            totals, target = carry
            logits = lax.dot_general(
                cat[shard, pl.ds(pl.multiple_of(b * ITEM_BLOCK, ITEM_BLOCK), ITEM_BLOCK), :],
                states[...],
                (((1,), (1,)), ((), ())),
                preferred_element_type=jnp.float32,
            )
            local = item_ids - (base + b * ITEM_BLOCK)
            matches = lax.broadcasted_iota(jnp.int32, logits.shape, 0) == local
            totals = totals + jnp.sum(jnp.exp(logits), axis=0, keepdims=True)
            target = target + jnp.sum(jnp.where(matches, logits, 0.0), axis=0, keepdims=True)
            return totals, target

        return lax.fori_loop(0, items // ITEM_BLOCK, block, carry)

    zero = jnp.zeros((1, nz * imps), jnp.float32)
    loads[6].wait()
    carry = score(0, c, (zero, zero))
    cat_copy().wait_recv()
    totals, target = score(1, other, carry)
    upper = lax.broadcasted_iota(jnp.int32, (8, LANES), 0) < 4
    for r in range(nz):
        cut = slice(r // 2 * LANES, (r // 2 + 1) * LANES)
        tile = jnp.where(upper, totals[:, cut], target[:, cut])
        stage[r] = pltpu.roll(tile, LANES - imps, 1) if r % 2 else tile

    def s_copy(r, dt):
        remote(
            stage.at[r], stats.at[line], s_send, s_recv, item=z_from(r), tensor=t_at(dt)
        ).start()

    each_line(s_copy)
    stats[line] = stage[0]

    each_z(1, lambda r: z_copy(r).wait_send())
    cat_copy().wait_send()
    for dt in range(1, nt):
        w_copy(dt, t).wait_send()
        ws_copy(dt, c).wait_send()
        each_z(1, lambda r: x_copy(r, dt, t).wait_send())
    each_line(lambda r, dt: g_copy(r, dt, t).wait_send())
    others = stats.at[0 : nlines - 1]
    all_stats = remote(others, others, s_send, s_recv, dp=other)
    all_stats.wait_recv()
    whole = jnp.sum(stats[...], axis=0)
    prop = whole[4:5, :] - jnp.log(whole[0:1, :])
    prop_out[...] = prop[:, :imps]
    all_stats.wait_send()


def local(events, lengths, packing, positions, logged, w_uvqk, w_out, catalogue):
    rows, width = events.shape
    imps = positions.shape[1]
    nz = lax.axis_size("item")
    nt = lax.axis_size("tensor")
    items = catalogue.shape[0]
    dma = pltpu.SemaphoreType.DMA
    vmem = pl.BlockSpec(memory_space=pltpu.VMEM)
    hbm = pl.BlockSpec(memory_space=pltpu.HBM)
    state, prop = pl.pallas_call(
        functools.partial(kernel, nz, nt),
        out_shape=(
            jax.ShapeDtypeStruct((imps, width // nt), jnp.bfloat16),
            jax.ShapeDtypeStruct((1, imps), jnp.float32),
        ),
        in_specs=[hbm] * 8,
        out_specs=(vmem, vmem),
        scratch_shapes=[
            pltpu.SMEM(packing.shape, jnp.int32),
            pltpu.SMEM(lengths.shape, jnp.int32),
            pltpu.VMEM(positions.shape, jnp.int32),
            pltpu.VMEM(logged.shape, jnp.int32),
            pltpu.VMEM((rows, width), jnp.bfloat16),
            pltpu.VMEM((width, 2 * DH), jnp.bfloat16),
            pltpu.VMEM((width, 2 * DH), jnp.bfloat16),
            pltpu.VMEM((nt * DH, width), jnp.bfloat16),
            pltpu.VMEM((2, items, width), jnp.bfloat16),
            pltpu.VMEM((nz * imps, width), jnp.bfloat16),
            pltpu.VMEM((nz * imps, nt * DH), jnp.bfloat16),
            pltpu.VMEM((nz * imps, width), jnp.bfloat16),
            pltpu.VMEM((1, nz * imps), jnp.int32),
            pltpu.VMEM((nz, 8, LANES), jnp.float32),
            pltpu.VMEM((nz * nt, 8, LANES), jnp.float32),
            dma((11,)),
            dma((nz,)),
            dma((nz,)),
            dma((nz * nt,)),
            dma((nz * nt,)),
            dma((nt,)),
            dma((nt,)),
            dma((nt,)),
            dma((nt,)),
            dma((nz * nt,)),
            dma((nz * nt,)),
            dma,
            dma,
            dma,
            dma,
        ],
        compiler_params=pltpu.CompilerParams(
            collective_id=0, has_side_effects=True, vmem_limit_bytes=63 * 1024 * 1024
        ),
        name="replay",
    )(packing, lengths, positions, logged, events, w_uvqk, w_out, catalogue)
    return state, prop.reshape(imps)


def solution(mesh):
    placed = (
        P(("groups", "item", "dp"), None),
        P("groups"),
        P("groups"),
        P("groups", None),
        P("groups", None),
        P(None, "tensor"),
        P("tensor", None),
        P(("item", "dp", "tensor"), None),
    )
    return jax.shard_map(
        local,
        mesh=mesh,
        in_specs=placed,
        out_specs=(P(("groups", "item", "dp"), "tensor"), P(("groups", "item", "dp"))),
        check_vma=False,
    )
```
